256 devices in a mesh: dp: 64 (over x, y, z_hi, core), mp: 4 (over z_lo).
Axes of the slice: x: 4, y: 4, z: 8 (z_hi: 2, z_lo: 4; z = z_hi * 4 + z_lo), core: 2. Of those that a mesh axis runs over, the one named last changes fastest.
Arguments:
- hidden: bfloat16 [32768, 16384], P('dp', 'mp'), may hold values from -64 to 64
- key_weight: bfloat16 [16384, 1024], P(('mp', 'dp')), may hold values from -0.046875 to 0.046875
- key_state: float32 [16384], P(('mp', 'dp')), may hold values from 2.9802323e-09 to 1.1920929e-07
- key_cotangent: bfloat16 [32768, 1024], P('dp'), may hold values from -6 to 6
- doc_lengths: int32 [128, 4], P('dp'), may hold values from 1 to 128, 256 in all within a row
Outputs:
- input_grad: bfloat16 [32768, 16384], P('dp', 'mp')
- new_weight: bfloat16 [16384, 1024], P(('mp', 'dp'))
- new_state: float32 [16384], P(('mp', 'dp'))
The draws below stay inside these ranges and needn't reach their ends.
Inputs may be any that keep to these rules, and one draw needn't show every extreme that they name: `doc_lengths`: each row lists the lengths of the documents of one sequence, in order, summing to 256.
All inputs are finite; a program needn't handle non-finite values.
Results may differ from the reference program's by a relative error of at most 0.0045.
Values may be sent and summed in bfloat16 or wider, within the bound.
No kernel may reach another device: no remote copies, remote signals or barrier semaphores. Data moves between devices by JAX's collectives and lax.ppermute only.
A program may use at most 128 MiB of HBM per device.

```python
import math
import jax
import jax.numpy as jnp
import numpy as np
from jax import lax

D = 16384
HD = 128
LEN = 256
DOCS = 4
KVW = 1024
MOST = 128
TOK_DEV = 512
SEQS = 128
TOKENS = 32768
ROWS_DEV = 64


def draw_hidden(key, part):
    draw_keys = jax.random.split(key, 5)
    base_draw = jax.random.normal(draw_keys[0], (TOKENS, D), jnp.float32)
    rising = 1.0 + 2.0 * jnp.arange(D, dtype=jnp.float32) / (D - 1)
    col_scale = jnp.exp(jax.random.uniform(draw_keys[1], (D,), jnp.float32, math.log(0.5), math.log(2.0)))
    row_scale = jnp.exp(jax.random.uniform(draw_keys[2], (TOKENS, 1), jnp.float32, math.log(0.5), math.log(2.0)))
    targets = jax.random.randint(draw_keys[4], (TOKENS // TOK_DEV,), 0, D // ROWS_DEV)
    token_block = jnp.arange(TOKENS) // TOK_DEV
    feature_block = jnp.arange(D) // ROWS_DEV
    amplified = 1.0 + 3.0 * (targets[token_block][:, None] == feature_block[None, :]).astype(jnp.float32)
    spiked = base_draw * row_scale * (col_scale * rising)[None, :] * amplified
    return jnp.clip(spiked, -64.0, 64.0).astype(jnp.bfloat16)


def level_of(stream_key, dims, shards, smallest, high):
    def one(axis_at, parts):
        steps = jax.random.uniform(jax.random.fold_in(jax.random.fold_in(stream_key, 6), axis_at), (parts,), jnp.float32, smallest / len(shards), high / len(shards))
        return jnp.repeat(jnp.exp(steps), dims[axis_at] // parts).reshape((-1,) + (1,) * (len(dims) - axis_at - 1))

    factor_of = one(*shards[0])
    for cut in shards[1:]:
        factor_of = factor_of * one(*cut)
    return factor_of


def split_up(count, total, bound, slope):
    portions = [(1 << 20) // math.isqrt(rank ** slope) + 1 for rank in range(2, count + 1)]
    rest, holding = total - bound - (count - 1), [1] * (count - 1)
    while rest > 0:
        free = [i for i in range(count - 1) if holding[i] < bound]
        pool, remaining = sum([portions[i] for i in free]), rest
        for i in free:
            addition = min(bound - holding[i], max(1, remaining * portions[i] // pool), rest)
            holding[i] = holding[i] + addition
            rest = rest - addition
    return np.array([bound] + holding)


def uneven(rng, number_of, total, bound, skew):
    if number_of == 2:
        one = jax.random.randint(rng, (), max(1, total - bound), min(bound, total - 1) + 1)
        return jnp.stack([one, total - one])
    tallies = jnp.asarray(split_up(number_of, total, bound, skew), jnp.int32)
    twos = (number_of - 1) // 2
    donor, sink = tallies[1:1 + 2 * twos:2], tallies[2:2 + 2 * twos:2]
    room = jnp.minimum(donor - 1, bound - sink)
    shifted = jax.random.randint(jax.random.fold_in(rng, 1), (twos,), 0, 1 << 20) % (room + 1)
    tallies = tallies.at[1:1 + 2 * twos:2].set(donor - shifted).at[2:2 + 2 * twos:2].set(sink + shifted)
    return tallies[jax.random.permutation(jax.random.fold_in(rng, 2), number_of)]


def normal_values(stream_key, shape, scale, reach, pieces=(), held_as=jnp.bfloat16):
    gain = level_of(stream_key, shape, pieces, -0.22, 0.18) if pieces else 1.0
    values = jax.random.normal(stream_key, shape, jnp.float32) * scale * gain
    return jnp.minimum(jnp.maximum(values, -reach), reach).astype(held_as)


def setup_inputs(seed: int = 0) -> dict:
    streams_of = jax.random.split(jax.random.key(seed), 6)
    return {
        "hidden": draw_hidden(jax.random.fold_in(streams_of[5], 71), 0),
        "key_weight": normal_values(streams_of[1], (D, KVW), D ** -0.5, 0.046875, ((0, 256),)),
        "key_state": jnp.clip(jnp.exp(math.log(1.1920928955078125e-07) - 3.6888794 * jax.random.uniform(streams_of[2], (D,), jnp.float32) ** level_of(streams_of[2], (D,), ((0, 256),), -0.2, 0.2)), 2.9802322831784522e-09, 1.1920928955078125e-07),
        "key_cotangent": normal_values(streams_of[3], (TOKENS, KVW), 1.0, 6.0, ((0, 64),)),
        "doc_lengths": jax.vmap(lambda own: uneven(own, DOCS, LEN, MOST, 1))(jax.random.split(streams_of[4], SEQS)).reshape((SEQS, DOCS)).astype(jnp.int32),
    }


learn_rate = 0.01

def positions_of(doc_lengths):
    doc_ends = jnp.cumsum(doc_lengths, axis=1).astype(jnp.int32)
    doc_starts = (doc_ends - doc_lengths).astype(jnp.int32)
    places = jnp.arange(LEN, dtype=jnp.int32)
    before = doc_starts[:, None, :] <= places[None, :, None]
    doc_start = lax.optimization_barrier(jnp.max(jnp.where(before, doc_starts[:, None, :], 0), axis=2)).astype(jnp.int32)
    return (places[None, :] - doc_start).reshape(-1).astype(jnp.int32)

def rope_back(cotangent, positions):
    half_dim = HD // 2
    frequency = jnp.exp(-(2.0 * jnp.arange(half_dim, dtype=jnp.float32) / HD) * jnp.log(jnp.float32(500000.0)))
    angles = positions.astype(jnp.float32)[:, None] * frequency[None, :]
    cos_part = jnp.cos(angles)[:, None, :]
    sin_part = jnp.sin(angles)[:, None, :]
    gradients = cotangent.astype(jnp.float32).reshape(cotangent.shape[0], -1, HD)
    first_half = gradients[..., :half_dim]
    second_half = gradients[..., half_dim:]
    rotated = jnp.concatenate([first_half * cos_part + second_half * sin_part, second_half * cos_part - first_half * sin_part], axis=-1)
    return rotated.reshape(cotangent.shape[0], -1).astype(jnp.bfloat16)

def reference(hidden, key_weight, key_state, key_cotangent, doc_lengths):
    positions = positions_of(doc_lengths)
    key_grad = rope_back(key_cotangent, positions)
    weight_grad = lax.dot_general(hidden, key_grad, (((0,), (0,)), ((), ())), preferred_element_type=jnp.float32)
    input_grad = lax.dot_general(key_grad, key_weight, (((1,), (1,)), ((), ())), preferred_element_type=jnp.float32).astype(jnp.bfloat16)
    squared = weight_grad * weight_grad
    squares_sum = jnp.sum(squared)
    clip_factor = jnp.minimum(jnp.float32(1.0), 1.0 / jnp.sqrt(squares_sum + 1e-06))
    row_mean = lax.optimization_barrier(jnp.mean(squared, axis=1))
    new_state = key_state + clip_factor * clip_factor * row_mean
    step_size = learn_rate * clip_factor * weight_grad / (jnp.sqrt(new_state)[:, None] + 1e-10)
    new_weight = (key_weight.astype(jnp.float32) - step_size).astype(jnp.bfloat16)
    return (input_grad, new_weight, new_state)
```

```python
import functools

import jax
import jax.numpy as jnp
from jax import lax
from jax.experimental import pallas as pl
from jax.experimental.pallas import tpu as pltpu
from jax.sharding import Mesh
from jax.sharding import PartitionSpec as P

HD = 128
LEN = 256
KVW = 1024
HALF = 512
DP = ("x", "y", "zh", "c")
MP_DP = ("mp", "x", "y", "zh", "c")
RATE = 0.01
BF = jnp.bfloat16
F32 = jnp.float32
VM = pl.BlockSpec(memory_space=pltpu.VMEM)
SM = pl.BlockSpec(memory_space=pltpu.SMEM)
ANY = pl.BlockSpec(memory_space=pl.ANY)
MIB = 1 << 20


def call(body, outs, in_specs, out_specs=None, scratch=(), vmem=40, flops=0, moved=0, alias=None):
    return pl.pallas_call(
        body,
        out_shape=outs,
        in_specs=in_specs,
        out_specs=[VM] * len(outs) if out_specs is None else out_specs,
        scratch_shapes=list(scratch),
        input_output_aliases=alias or {},
        compiler_params=pltpu.CompilerParams(vmem_limit_bytes=vmem * MIB),
        cost_estimate=pl.CostEstimate(flops=flops, bytes_accessed=moved, transcendentals=0),
    )


def struct(shape, dtype):
    return jax.ShapeDtypeStruct(shape, dtype)


def shift(value, axis, by):
    size = lax.axis_size(axis)
    return lax.ppermute(value, axis, [(i, (i + by) % size) for i in range(size)])


def swap_cores(value):
    return lax.ppermute(value, "c", [(0, 1), (1, 0)])


def rope_kernel(len_ref, cot_ref, grad_ref, turned_ref):
    lane = lax.broadcasted_iota(jnp.int32, (LEN, HD), 1)
    place = lax.broadcasted_iota(jnp.int32, (LEN, HD), 0)
    index = jnp.where(lane < HD // 2, lane, lane - HD // 2).astype(F32)
    frequency = jnp.exp(-(2.0 * index / HD) * jnp.log(jnp.full((LEN, HD), 500000.0, F32)))
    for seq in range(2):
        start = jnp.int32(0)
        first = jnp.zeros((LEN, HD), jnp.int32)
        for doc in range(1, 4):
            start = start + len_ref[seq, doc - 1]
            first = jnp.where(place >= start, start, first)
        angle = (place - first).astype(F32) * frequency
        cos = jnp.cos(angle)
        sin = jnp.sin(angle)
        sin = jnp.where(lane < HD // 2, sin, -sin)
        rows = pl.ds(seq * LEN, LEN)
        for head in range(KVW // HD):
            cols = pl.ds(head * HD, HD)
            value = cot_ref[rows, cols].astype(F32)
            out = value * cos + pltpu.roll(value, HD // 2, 1) * sin
            grad_ref[rows, cols] = out.astype(BF)
            turned_ref[cols, rows] = out.T.astype(BF)


def rope(doc_lengths, cotangent):
    return call(
        rope_kernel,
        [struct((512, KVW), BF), struct((KVW, 512), BF)],
        [SM, VM],
        moved=3 * MIB,
    )(doc_lengths, cotangent)


def pick_kernel(core_ref, hidden_ref, out_ref, sem):
    other = 1 - core_ref[0]
    copies = [
        pltpu.make_async_copy(
            hidden_ref.at[:, pl.ds(pl.multiple_of((2 * j + other) * 128, 128), 128)],
            out_ref.at[:, pl.ds(j * 128, 128)],
            sem.at[j],
        )
        for j in range(16)
    ]
    for copy in copies:
        copy.start()
    for copy in copies:
        copy.wait()


def pick(core, hidden):
    return call(
        pick_kernel,
        [struct((512, 2048), BF)],
        [SM, ANY],
        scratch=[pltpu.SemaphoreType.DMA((16,))],
        moved=4 * MIB,
    )(core, hidden)[0]


def grad_kernel(at_ref, own_t, other_t, other_h, hidden_ref, *refs):
    a_out, b_out = refs[:4], refs[4:8]
    mine, sem = refs[8:]
    x, y, core = at_ref[0], at_ref[1], at_ref[2]
    copies = [
        pltpu.make_async_copy(
            hidden_ref.at[:, pl.ds(pl.multiple_of((2 * j + core) * 128, 128), 128)],
            mine.at[:, pl.ds(j * 128, 128)],
            sem.at[j],
        )
        for j in range(16)
    ]
    for copy in copies:
        copy.start()
    for copy in copies:
        copy.wait()
    for j in (2, 1, 3, 0):
        to = lax.rem(x + j, 4)
        cols = pl.ds(pl.multiple_of(to * 512, 512), 512)
        out = jnp.dot(own_t[:HALF, :], mine[:, cols], preferred_element_type=F32)
        out += jnp.dot(other_t[:HALF, :], other_h[:, cols], preferred_element_type=F32)
        a_out[j][...] = out.astype(a_out[j].dtype)
        to = lax.rem(y + j, 4)
        tiles = [pl.ds(pl.multiple_of((4 * i + to) * 128, 128), 128) for i in range(4)]
        left = jnp.concatenate([mine[:, t] for t in tiles], axis=1)
        right = jnp.concatenate([other_h[:, t] for t in tiles], axis=1)
        out = jnp.dot(own_t[HALF:, :], left, preferred_element_type=F32)
        out += jnp.dot(other_t[HALF:, :], right, preferred_element_type=F32)
        b_out[j][...] = out.astype(b_out[j].dtype)


def grad_parts(at, own_t, other_t, other_h, hidden):
    kinds = [struct((HALF, 512), F32)] + [struct((HALF, 512), BF)] * 3
    outs = call(
        grad_kernel,
        kinds + kinds,
        [SM, VM, VM, VM, ANY],
        scratch=[pltpu.VMEM((512, 2048), BF), pltpu.SemaphoreType.DMA((16,))],
        flops=2 * 1024 * 1024 * 2048,
        moved=11 * MIB,
    )(at, own_t, other_t, other_h, hidden)
    return outs[:4], outs[4:]


def first_sum_kernel(at_ref, *refs):
    a_in, b_in = refs[:4], refs[4:8]
    outs = (refs[8:12], refs[12:16])
    for side, (held, out) in enumerate(zip((a_in, b_in), outs)):
        me = at_ref[1 - side]
        for j in range(4):
            to = lax.rem(me + j, 4)
            cols = pl.ds(pl.multiple_of(to * 128, 128), 128)
            total = held[0][:, cols]
            for ref in held[1:]:
                total += ref[:, cols].astype(F32)
            out[j][...] = total.astype(out[j].dtype)


def first_sum(at, a_parts, b_parts):
    kinds = [struct((HALF, 128), F32)] + [struct((HALF, 128), BF)] * 3
    outs = call(
        first_sum_kernel, kinds + kinds, [SM] + [VM] * 8, moved=6 * MIB
    )(at, *a_parts, *b_parts)
    return outs[:4], outs[4:]


def second_sum_kernel(at_ref, *refs):
    q_out, p_out, local_out = refs[8:11]
    full = refs[11]
    zh, core = at_ref[3], at_ref[2]
    for side in range(2):
        held = refs[4 * side : 4 * side + 4]
        total = held[0][...]
        for ref in held[1:]:
            total += ref[...].astype(F32)
        full[:, pl.ds(side * HALF, HALF)] = total.T
    mine = full[pl.ds(pl.multiple_of(core * 64, 64), 64), :]
    other = full[pl.ds(pl.multiple_of((1 - core) * 64, 64), 64), :]
    straight = zh == core
    q_out[...] = jnp.where(straight, other, mine).astype(BF)
    p_out[...] = other.astype(BF)
    local_out[...] = jnp.where(straight, mine, 0.0)


def second_sum(at, a_parts, b_parts):
    return call(
        second_sum_kernel,
        [struct((64, KVW), BF), struct((64, KVW), BF), struct((64, KVW), F32)],
        [SM] + [VM] * 8,
        scratch=[pltpu.VMEM((128, KVW), F32)],
        moved=2 * MIB,
    )(at, *a_parts, *b_parts)


def third_sum_kernel(local, q_in, p_in, grad_out, rows_out, total_out):
    grad = local[...] + (q_in[...].astype(F32) + p_in[...].astype(F32))
    grad_out[...] = grad
    rows = jnp.sum(grad * grad, axis=1, keepdims=True)
    rows_out[...] = jnp.broadcast_to(rows, (64, 128))
    total = jnp.sum(rows, axis=0, keepdims=True)
    total_out[...] = jnp.broadcast_to(total, (8, 128))


def third_sum(local, q_in, p_in):
    return call(
        third_sum_kernel,
        [struct((64, KVW), F32), struct((64, 128), F32), struct((8, 128), F32)],
        [VM] * 3,
        moved=MIB,
    )(local, q_in, p_in)


def spread_sum(value, axes):
    size = lax.axis_size(axes)
    copies = jnp.broadcast_to(value[None], (size, *value.shape))
    return jnp.sum(lax.all_to_all(copies, axes, 0, 0, tiled=True), axis=0)


def update_kernel(total, rows, grad, weight, state, weight_out, state_out):
    squares = total[0:1, 0:1]
    clip = jnp.minimum(1.0, 1.0 / jnp.sqrt(squares + 1e-06))
    row = lax.broadcasted_iota(jnp.int32, (64, 64), 0)
    col = lax.broadcasted_iota(jnp.int32, (64, 64), 1)
    eye = row == col
    held = jnp.sum(jnp.where(eye, state[...], 0.0), axis=1, keepdims=True)
    new = held + clip * clip * (rows[:, 0:1] * (1.0 / KVW))
    state_out[...] = jnp.sum(jnp.where(eye, new, 0.0), axis=0, keepdims=True)
    step = RATE * clip * grad[...] / (jnp.sqrt(new) + 1e-10)
    weight_out[...] = (weight[...].astype(F32) - step).astype(BF)


def update(total, rows, grad, weight, state):
    new_weight, new_state = call(
        update_kernel,
        [struct((64, KVW), BF), struct((1, 64), F32)],
        [VM] * 5,
        moved=MIB,
    )(total, rows, grad, weight, state.reshape(1, 64))
    return new_weight, new_state.reshape(64)


def input_kernel(at_ref, grad_ref, *refs):
    a_own, b_own, a_far, b_far = refs[:4], refs[4:8], refs[8:12], refs[12:16]
    out = refs[16]
    x, y, core = at_ref[0], at_ref[1], at_ref[2]
    for k in range(4):
        for j in range(4):
            row = lax.rem(x + 4 - j, 4) * 4 + lax.rem(y + 4 - k, 4)
            for a, b, at in ((a_own, b_own, core), (a_far, b_far, 1 - core)):
                weight = jnp.concatenate([a[k][j], b[j][k]], axis=0)
                value = lax.dot_general(
                    grad_ref[...],
                    weight,
                    (((1,), (1,)), ((), ())),
                    preferred_element_type=F32,
                )
                cols = pl.ds(pl.multiple_of((2 * row + at) * 128, 128), 128)
                out[:, cols] = value.astype(BF)


def input_product(at, key_grad, pieces):
    return call(
        input_kernel,
        [struct((512, 4096), BF)],
        [SM] + [VM] * 17,
        flops=2 * 512 * 1024 * 4096,
        moved=13 * MIB,
    )(at, key_grad, *pieces)[0]


def shards(hidden, key_weight, key_state, key_cotangent, doc_lengths):
    x, y, zh, core = (lax.axis_index(name) for name in DP)
    at = jnp.stack([x, y, core, zh]).astype(jnp.int32)
    straight = zh == core

    other_h = swap_cores(pick(at[2:3], hidden))
    key_grad, turned = rope(doc_lengths, key_cotangent)
    other_t = swap_cores(turned)

    q_w = lax.ppermute(key_weight, ("zh", "c"), [(0, 2), (1, 0), (2, 3), (3, 1)])
    p_w = lax.ppermute(key_weight, ("zh", "c"), [(1, 2), (2, 1)])
    same = jnp.where(straight, key_weight, q_w)
    cross = jnp.where(straight, q_w, p_w)
    rows_a = jnp.where(core == 0, same, cross)
    rows_b = jnp.where(core == 0, cross, same)
    ring_a = [rows_a] + [shift(rows_a, "x", j) for j in (1, 2, 3)]
    ring_b = [rows_b] + [shift(rows_b, "y", j) for j in (1, 2, 3)]

    a_parts, b_parts = grad_parts(at, turned, other_t, other_h, hidden)
    a_parts = [a_parts[0]] + [shift(a_parts[j], "x", j) for j in (1, 2, 3)]
    b_parts = [b_parts[0]] + [shift(b_parts[j], "y", j) for j in (1, 2, 3)]
    a_next, b_next = first_sum(at, a_parts, b_parts)
    a_next = [a_next[0]] + [shift(a_next[j], "y", j) for j in (1, 2, 3)]
    b_next = [b_next[0]] + [shift(b_next[j], "x", j) for j in (1, 2, 3)]
    q_out, p_out, local = second_sum(at, a_next, b_next)
    q_in = lax.ppermute(q_out, ("zh", "c"), [(0, 1), (1, 3), (2, 0), (3, 2)])
    p_in = lax.ppermute(p_out, ("zh", "c"), [(2, 1), (1, 2)])
    grad, rows, total = third_sum(local, q_in, p_in)

    total = lax.psum(total, "c")
    total = spread_sum(total, ("x", "y"))
    total = spread_sum(total, ("zh", "mp"))
    new_weight, new_state = update(total, rows, grad, key_weight, key_state)

    cat_a = jnp.stack(ring_a)
    cat_b = jnp.stack(ring_b)
    full_a = [cat_a] + [shift(cat_a, "y", j) for j in (1, 2, 3)]
    full_b = [cat_b] + [shift(cat_b, "x", j) for j in (1, 2, 3)]
    far_a = [swap_cores(v) for v in full_a]
    far_b = [swap_cores(v) for v in full_b]
    input_grad = input_product(at, key_grad, [*full_a, *full_b, *far_a, *far_b])
    return (input_grad, new_weight, new_state)


def solution(mesh):
    finer = Mesh(mesh.devices.reshape(4, 4, 2, 2, mesh.shape["mp"]), (*DP, "mp"))
    placed = (P(DP, "mp"), P(MP_DP, None), P(MP_DP), P(DP, None), P(DP, None))
    return jax.shard_map(
        shards,
        mesh=finer,
        in_specs=placed,
        out_specs=(P(DP, "mp"), P(MP_DP, None), P(MP_DP)),
        check_vma=False,
    )
```

```python
import functools

import jax
import jax.numpy as jnp
from jax import lax
from jax.experimental import pallas as pl
from jax.experimental.pallas import tpu as pltpu
from jax.sharding import Mesh
from jax.sharding import PartitionSpec as P

HD = 128
LEN = 256
KVW = 1024
HALF = 512
DP = ("x", "y", "zh", "c")
MP_DP = ("mp", "x", "y", "zh", "c")
RATE = 0.01
BF = jnp.bfloat16
F32 = jnp.float32
VM = pl.BlockSpec(memory_space=pltpu.VMEM)
SM = pl.BlockSpec(memory_space=pltpu.SMEM)
ANY = pl.BlockSpec(memory_space=pl.ANY)
MIB = 1 << 20


def call(body, outs, in_specs, out_specs=None, scratch=(), vmem=8, flops=0, moved=0, alias=None):
    return pl.pallas_call(
        body,
        out_shape=outs,
        in_specs=in_specs,
        out_specs=[VM] * len(outs) if out_specs is None else out_specs,
        scratch_shapes=list(scratch),
        input_output_aliases=alias or {},
        compiler_params=pltpu.CompilerParams(vmem_limit_bytes=vmem * MIB),
        cost_estimate=pl.CostEstimate(flops=flops, bytes_accessed=moved, transcendentals=0),
    )


def struct(shape, dtype):
    return jax.ShapeDtypeStruct(shape, dtype)


def spread(value, by):
    pairs = []
    for x in range(4):
        for y in range(4):
            here = (4 * x + y) * 2
            pairs.append((here, (4 * ((x + by) % 4) + y) * 2))
            pairs.append((here + 1, (4 * x + (y + by) % 4) * 2 + 1))
    return lax.ppermute(value, ("x", "y", "c"), pairs)


def spread_across(value, by):
    pairs = []
    for x in range(4):
        for y in range(4):
            here = (4 * x + y) * 2
            pairs.append((here, (4 * x + (y + by) % 4) * 2))
            pairs.append((here + 1, (4 * ((x + by) % 4) + y) * 2 + 1))
    return lax.ppermute(value, ("x", "y", "c"), pairs)


def swap_cores(value):
    return lax.ppermute(value, "c", [(0, 1), (1, 0)])


def rope_kernel(len_ref, cot_ref, grad_ref, turned_ref):
    lane = lax.broadcasted_iota(jnp.int32, (LEN, HD), 1)
    place = lax.broadcasted_iota(jnp.int32, (LEN, HD), 0)
    index = jnp.where(lane < HD // 2, lane, lane - HD // 2).astype(F32)
    frequency = jnp.exp(-(2.0 * index / HD) * jnp.log(jnp.full((LEN, HD), 500000.0, F32)))
    row = lax.broadcasted_iota(jnp.int32, (HD, HD), 0)
    col = lax.broadcasted_iota(jnp.int32, (HD, HD), 1)
    eye = (row == col).astype(F32).astype(BF)
    far = jnp.where(col < HD // 2, col + HD // 2, col - HD // 2)
    swap = (row == far).astype(F32).astype(BF)
    for seq in range(2):
        start = jnp.int32(0)
        first = jnp.zeros((LEN, HD), jnp.int32)
        for doc in range(1, 4):
            start = start + len_ref[seq, doc - 1]
            first = jnp.where(place >= start, start, first)
        angle = (place - first).astype(F32) * frequency
        cos = jnp.cos(angle)
        sin = jnp.sin(angle)
        sin = jnp.where(lane < HD // 2, sin, -sin)
        rows = pl.ds(seq * LEN, LEN)
        for head in range(KVW // HD):
            cols = pl.ds(head * HD, HD)
            value = cot_ref[rows, cols]
            swapped = jnp.dot(value, swap, preferred_element_type=F32)
            out = (value.astype(F32) * cos + swapped * sin).astype(BF)
            grad_ref[rows, cols] = out
            turned = lax.dot_general(
                eye, out, (((1,), (1,)), ((), ())), preferred_element_type=F32
            )
            turned_ref[cols, rows] = turned.astype(BF)


def rope(doc_lengths, cotangent):
    return call(
        rope_kernel,
        [struct((512, KVW), BF), struct((KVW, 512), BF)],
        [SM, VM],
        vmem=12,
        moved=3 * MIB,
    )(doc_lengths, cotangent)


def split_kernel(at_ref, hidden_ref, mine, other):
    core = at_ref[2]
    for j in range(16):
        here = pl.ds(j * 128, 128)
        mine[:, here] = hidden_ref[:, pl.ds(pl.multiple_of((2 * j + core) * 128, 128), 128)]
        other[:, here] = hidden_ref[:, pl.ds(pl.multiple_of((2 * j + 1 - core) * 128, 128), 128)]


def split(at, hidden):
    half = pl.BlockSpec((256, 2048), lambda i: (i, 0))
    return pl.pallas_call(
        split_kernel,
        grid=(2,),
        in_specs=[SM, pl.BlockSpec((256, 4096), lambda i: (i, 0))],
        out_specs=[half, half],
        out_shape=[struct((512, 2048), BF)] * 2,
        compiler_params=pltpu.CompilerParams(vmem_limit_bytes=16 * MIB),
        cost_estimate=pl.CostEstimate(flops=0, bytes_accessed=8 * MIB, transcendentals=0),
    )(at, hidden)


def tile(at_ref, first, second):
    core = at_ref[2]
    return first * jnp.where(core == 0, 4, 1) + second * jnp.where(core == 0, 1, 4)


def grad_kernel(steps, at_ref, own_t, other_t, mine, other_h, *outs):
    first = at_ref[0]
    for j, out in zip(steps, outs):
        to = lax.rem(first + j, 4)
        tiles = [pl.ds(pl.multiple_of(tile(at_ref, to, i) * 128, 128), 128) for i in range(4)]
        for half in (0, 1):
            pair = tiles[2 * half : 2 * half + 2]
            right = jnp.concatenate(
                [jnp.concatenate([h[:, t] for t in pair], axis=1) for h in (mine, other_h)],
                axis=0,
            )
            for part in (0, 1):
                rows = slice(part * HALF, part * HALF + HALF)
                left = jnp.concatenate([own_t[rows, :], other_t[rows, :]], axis=1)
                value = jnp.dot(left, right, preferred_element_type=F32)
                out[rows, half * 256 : half * 256 + 256] = value.astype(out.dtype)


def grad_parts(steps, at, own_t, other_t, mine, other_h):
    outs = [struct((KVW, 512), BF if j else F32) for j in steps]
    return call(
        functools.partial(grad_kernel, steps),
        outs,
        [SM, VM, VM, VM, VM],
        vmem=20,
        flops=2 * 1024 * 512 * 1024 * len(steps),
        moved=8 * MIB,
    )(at, own_t, other_t, mine, other_h)


def first_sum_kernel(at_ref, *refs):
    held, outs = refs[:4], refs[4:]
    for j in range(4):
        cols = pl.ds(pl.multiple_of(lax.rem(at_ref[1] + j, 4) * 128, 128), 128)
        total = held[0][:, cols]
        for ref in held[1:]:
            total += ref[:, cols].astype(F32)
        outs[j][...] = total.astype(outs[j].dtype)


def first_sum(at, parts):
    kinds = [struct((KVW, 128), F32)] + [struct((KVW, 128), BF)] * 3
    return call(first_sum_kernel, kinds, [SM] + [VM] * 4, vmem=14, moved=6 * MIB)(at, *parts)


def second_sum_kernel(at_ref, *refs):
    held = refs[:4]
    q_out, p_out, local_out, full = refs[4:]
    zh, core = at_ref[3], at_ref[2]
    total = held[0][...]
    for ref in held[1:]:
        total += ref[...].astype(F32)
    full[...] = total.T
    mine = full[pl.ds(pl.multiple_of(core * 64, 64), 64), :]
    other = full[pl.ds(pl.multiple_of((1 - core) * 64, 64), 64), :]
    straight = zh == core
    q_out[...] = jnp.where(straight, other, mine).astype(BF)
    p_out[...] = other.astype(BF)
    local_out[...] = jnp.where(straight, mine, 0.0)


def second_sum(at, parts):
    return call(
        second_sum_kernel,
        [struct((64, KVW), BF), struct((64, KVW), BF), struct((64, KVW), F32)],
        [SM] + [VM] * 4,
        scratch=[pltpu.VMEM((128, KVW), F32)],
        moved=2 * MIB,
    )(at, *parts)


def third_sum_kernel(local, q_in, p_in, grad_out, rows_out, total_out):
    grad = local[...] + (q_in[...].astype(F32) + p_in[...].astype(F32))
    grad_out[...] = grad
    rows = jnp.sum(grad * grad, axis=1, keepdims=True)
    rows_out[...] = jnp.broadcast_to(rows, (64, 128))
    total = jnp.sum(rows, axis=0, keepdims=True)
    total_out[...] = jnp.broadcast_to(total, (8, 128))


def third_sum(local, q_in, p_in):
    return call(
        third_sum_kernel,
        [struct((64, KVW), F32), struct((64, 128), F32), struct((8, 128), F32)],
        [VM] * 3,
        moved=MIB,
    )(local, q_in, p_in)


def send_all(value, axes):
    copies = jnp.broadcast_to(value[None], (lax.axis_size(axes), *value.shape))
    return lax.all_to_all(copies, axes, 0, 0, tiled=True)


def spread_sum(value, axes):
    return jnp.sum(send_all(value, axes), axis=0)


def update_kernel(total, rows, grad, weight, state, weight_out, state_out):
    squares = total[0:1, 0:1]
    clip = jnp.minimum(1.0, 1.0 / jnp.sqrt(squares + 1e-06))
    row = lax.broadcasted_iota(jnp.int32, (64, 64), 0)
    col = lax.broadcasted_iota(jnp.int32, (64, 64), 1)
    eye = row == col
    held = jnp.sum(jnp.where(eye, state[...], 0.0), axis=1, keepdims=True)
    new = held + clip * clip * (rows[:, 0:1] * (1.0 / KVW))
    state_out[...] = jnp.sum(jnp.where(eye, new, 0.0), axis=0, keepdims=True)
    step = RATE * clip * grad[...] / (jnp.sqrt(new) + 1e-10)
    weight_out[...] = (weight[...].astype(F32) - step).astype(BF)


def update(total, rows, grad, weight, state):
    new_weight, new_state = call(
        update_kernel,
        [struct((64, KVW), BF), struct((1, 64), F32)],
        [VM] * 5,
        moved=MIB,
    )(total, rows, grad, weight, state.reshape(1, 64))
    return new_weight, new_state.reshape(64)


def input_kernel(at_ref, grad_ref, *refs):
    own, far = refs[:4], refs[4:8]
    out, held, sem = refs[8:]
    first, second, core = at_ref[0], at_ref[1], at_ref[2]
    order = sorted(((k, j) for k in range(4) for j in range(4)), key=lambda t: (max(t), t))
    copies = []
    for n, (k, j) in enumerate(order):
        weight = jnp.concatenate([own[k][j], far[j][k]], axis=0)
        value = lax.dot_general(
            grad_ref[...], weight, (((1,), (1,)), ((), ())), preferred_element_type=F32
        ).astype(BF)
        row = tile(at_ref, lax.rem(first + 4 - j, 4), lax.rem(second + 4 - k, 4))
        for i, side in enumerate((core, 1 - core)):
            held[n, i] = value[:, i * 128 : i * 128 + 128]
            cols = pl.ds(pl.multiple_of((2 * row + side) * 128, 128), 128)
            copy = pltpu.make_async_copy(held.at[n, i], out.at[:, cols], sem.at[2 * n + i])
            copy.start()
            copies.append(copy)
    for copy in copies:
        copy.wait()


def input_product(at, key_grad, own, far):
    return call(
        input_kernel,
        [struct((512, 4096), BF)],
        [SM] + [VM] * 9,
        out_specs=[ANY],
        scratch=[pltpu.VMEM((16, 2, 512, 128), BF), pltpu.SemaphoreType.DMA((32,))],
        vmem=22,
        flops=2 * 512 * 1024 * 4096,
        moved=13 * MIB,
    )(at, key_grad, *own, *far)[0]


def shards(hidden, key_weight, key_state, key_cotangent, doc_lengths):
    x, y, zh, core = (lax.axis_index(name) for name in DP)
    first = jnp.where(core == 0, x, y)
    second = jnp.where(core == 0, y, x)
    at = jnp.stack([first, second, core, zh]).astype(jnp.int32)
    straight = zh == core

    mine, other_h = split(at, hidden)
    other_h = swap_cores(other_h)
    key_grad, turned = rope(doc_lengths, key_cotangent)
    other_t = swap_cores(turned)

    part2, part1 = grad_parts((2, 1), at, turned, other_t, mine, other_h)
    part3, part0 = grad_parts((3, 0), at, turned, other_t, mine, other_h)
    parts = [part0] + [spread(v, j) for j, v in ((1, part1), (2, part2), (3, part3))]

    weight, _ = lax.optimization_barrier((key_weight, part0))
    q_w = lax.ppermute(weight, ("zh", "c"), [(0, 2), (1, 0), (2, 3), (3, 1)])
    p_w = lax.ppermute(weight, ("zh", "c"), [(1, 2), (2, 1)])
    same = jnp.where(straight, key_weight, q_w)
    cross = jnp.where(straight, q_w, p_w)
    rows = jnp.concatenate(
        [jnp.where(core == 0, same, cross), jnp.where(core == 0, cross, same)], axis=0
    )

    near = [spread(rows, 1), spread(rows, 3)]
    parts[0], rows, *near = lax.optimization_barrier((parts[0], rows, *near))

    sums = first_sum(at, parts)
    ring = [rows, near[0], spread(rows, 2), near[1]]
    sums = [sums[0]] + [spread_across(sums[j], j) for j in (1, 2, 3)]
    q_out, p_out, local = second_sum(at, sums)
    q_in = lax.ppermute(q_out, ("zh", "c"), [(0, 1), (1, 3), (2, 0), (3, 2)])
    p_in = lax.ppermute(p_out, ("zh", "c"), [(2, 1), (1, 2)])

    *ring, _ = lax.optimization_barrier((*ring, q_out))
    cat = jnp.stack(ring)
    own = [cat] + [spread_across(cat, j) for j in (1, 2, 3)]

    grad, squares, total = third_sum(local, q_in, p_in)
    far = [swap_cores(cat)]
    total = lax.psum(total, "c")
    total = spread_sum(total, ("zh", "mp"))
    *rest, total = lax.optimization_barrier((*own[1:], total))
    far += [swap_cores(v) for v in rest]
    own = [cat, *rest]
    everywhere = send_all(total, ("x", "y"))
    input_grad = input_product(at, key_grad, own, far)
    input_grad, everywhere = lax.optimization_barrier((input_grad, everywhere))
    total = jnp.sum(everywhere, axis=0)
    new_weight, new_state = update(total, squares, grad, key_weight, key_state)
    return (input_grad, new_weight, new_state)


def solution(mesh):
    finer = Mesh(mesh.devices.reshape(4, 4, 2, 2, mesh.shape["mp"]), (*DP, "mp"))
    placed = (P(DP, "mp"), P(MP_DP, None), P(MP_DP), P(DP, None), P(DP, None))
    return jax.shard_map(
        shards,
        mesh=finer,
        in_specs=placed,
        out_specs=(P(DP, "mp"), P(MP_DP, None), P(MP_DP)),
        check_vma=False,
    )
```

```python
import functools

import jax
import jax.numpy as jnp
from jax import lax
from jax.experimental import pallas as pl
from jax.experimental.pallas import tpu as pltpu
from jax.sharding import Mesh
from jax.sharding import PartitionSpec as P

HD = 128
LEN = 256
KVW = 1024
HALF = 512
DP = ("x", "y", "zh", "c")
MP_DP = ("mp", "x", "y", "zh", "c")
RATE = 0.01
BF = jnp.bfloat16
F32 = jnp.float32
VM = pl.BlockSpec(memory_space=pltpu.VMEM)
SM = pl.BlockSpec(memory_space=pltpu.SMEM)
ANY = pl.BlockSpec(memory_space=pl.ANY)
MIB = 1 << 20


def call(body, outs, in_specs, out_specs=None, scratch=(), vmem=8, flops=0, moved=0, alias=None):
    return pl.pallas_call(
        body,
        out_shape=outs,
        in_specs=in_specs,
        out_specs=[VM] * len(outs) if out_specs is None else out_specs,
        scratch_shapes=list(scratch),
        input_output_aliases=alias or {},
        compiler_params=pltpu.CompilerParams(vmem_limit_bytes=vmem * MIB),
        cost_estimate=pl.CostEstimate(flops=flops, bytes_accessed=moved, transcendentals=0),
    )


def struct(shape, dtype):
    return jax.ShapeDtypeStruct(shape, dtype)


def spread(value, by):
    pairs = []
    for x in range(4):
        for y in range(4):
            here = (4 * x + y) * 2
            pairs.append((here, (4 * ((x + by) % 4) + y) * 2))
            pairs.append((here + 1, (4 * x + (y + by) % 4) * 2 + 1))
    return lax.ppermute(value, ("x", "y", "c"), pairs)


def spread_across(value, by):
    pairs = []
    for x in range(4):
        for y in range(4):
            here = (4 * x + y) * 2
            pairs.append((here, (4 * x + (y + by) % 4) * 2))
            pairs.append((here + 1, (4 * ((x + by) % 4) + y) * 2 + 1))
    return lax.ppermute(value, ("x", "y", "c"), pairs)


def swap_cores(value):
    return lax.ppermute(value, "c", [(0, 1), (1, 0)])


def rope_kernel(len_ref, cot_ref, turned_ref):
    lane = lax.broadcasted_iota(jnp.int32, (LEN, HD), 1)
    place = lax.broadcasted_iota(jnp.int32, (LEN, HD), 0)
    index = jnp.where(lane < HD // 2, lane, lane - HD // 2).astype(F32)
    frequency = jnp.exp(-(2.0 * index / HD) * jnp.log(jnp.full((LEN, HD), 500000.0, F32)))
    row = lax.broadcasted_iota(jnp.int32, (HD, HD), 0)
    col = lax.broadcasted_iota(jnp.int32, (HD, HD), 1)
    eye = (row == col).astype(F32).astype(BF)
    far = jnp.where(col < HD // 2, col + HD // 2, col - HD // 2)
    swap = (row == far).astype(F32).astype(BF)
    for seq in range(2):
        start = jnp.int32(0)
        first = jnp.zeros((LEN, HD), jnp.int32)
        for doc in range(1, 4):
            start = start + len_ref[seq, doc - 1]
            first = jnp.where(place >= start, start, first)
        angle = (place - first).astype(F32) * frequency
        cos = jnp.cos(angle)
        sin = jnp.sin(angle)
        sin = jnp.where(lane < HD // 2, sin, -sin)
        rows = pl.ds(seq * LEN, LEN)
        for head in range(KVW // HD):
            cols = pl.ds(head * HD, HD)
            value = cot_ref[rows, cols]
            swapped = jnp.dot(value, swap, preferred_element_type=F32)
            out = (value.astype(F32) * cos + swapped * sin).astype(BF)
            turned = lax.dot_general(
                eye, out, (((1,), (1,)), ((), ())), preferred_element_type=F32
            )
            turned_ref[cols, rows] = turned.astype(BF)


def rope(doc_lengths, cotangent):
    return call(
        rope_kernel,
        [struct((KVW, 512), BF)],
        [SM, VM],
        vmem=12,
        moved=3 * MIB,
    )(doc_lengths, cotangent)[0]


def turn_back_kernel(turned_ref, grad_ref):
    row = lax.broadcasted_iota(jnp.int32, (256, 256), 0)
    col = lax.broadcasted_iota(jnp.int32, (256, 256), 1)
    eye = (row == col).astype(F32).astype(BF)
    for seq in range(2):
        rows = slice(seq * LEN, seq * LEN + LEN)
        value = lax.dot_general(
            eye, turned_ref[:, rows], (((1,), (1,)), ((), ())), preferred_element_type=F32
        )
        grad_ref[rows, :] = value.astype(BF)


def turn_back(turned):
    return call(
        turn_back_kernel, [struct((512, KVW), BF)], [VM], vmem=12, moved=2 * MIB
    )(turned)[0]


def split_kernel(at_ref, hidden_ref, mine, other):
    core = at_ref[2]
    for j in range(16):
        here = pl.ds(j * 128, 128)
        mine[:, here] = hidden_ref[:, pl.ds(pl.multiple_of((2 * j + core) * 128, 128), 128)]
        other[:, here] = hidden_ref[:, pl.ds(pl.multiple_of((2 * j + 1 - core) * 128, 128), 128)]


def split(at, hidden):
    half = pl.BlockSpec((256, 2048), lambda i: (i, 0))
    return pl.pallas_call(
        split_kernel,
        grid=(2,),
        in_specs=[SM, pl.BlockSpec((256, 4096), lambda i: (i, 0))],
        out_specs=[half, half],
        out_shape=[struct((512, 2048), BF)] * 2,
        compiler_params=pltpu.CompilerParams(vmem_limit_bytes=16 * MIB),
        cost_estimate=pl.CostEstimate(flops=0, bytes_accessed=8 * MIB, transcendentals=0),
    )(at, hidden)


def tile(at_ref, first, second):
    core = at_ref[2]
    return first * jnp.where(core == 0, 4, 1) + second * jnp.where(core == 0, 1, 4)


def grad_kernel(steps, at_ref, own_t, other_t, mine, other_h, *outs):
    first = at_ref[0]
    for j, out in zip(steps, outs):
        to = lax.rem(first + j, 4)
        tiles = [pl.ds(pl.multiple_of(tile(at_ref, to, i) * 128, 128), 128) for i in range(4)]
        for half in (0, 1):
            pair = tiles[2 * half : 2 * half + 2]
            right = jnp.concatenate(
                [jnp.concatenate([h[:, t] for t in pair], axis=1) for h in (mine, other_h)],
                axis=0,
            )
            for part in (0, 1):
                rows = slice(part * HALF, part * HALF + HALF)
                left = jnp.concatenate([own_t[rows, :], other_t[rows, :]], axis=1)
                value = jnp.dot(left, right, preferred_element_type=F32)
                out[rows, half * 256 : half * 256 + 256] = value.astype(out.dtype)


def grad_parts(steps, at, own_t, other_t, mine, other_h):
    outs = [struct((KVW, 512), BF if j else F32) for j in steps]
    return call(
        functools.partial(grad_kernel, steps),
        outs,
        [SM, VM, VM, VM, VM],
        vmem=20,
        flops=2 * 1024 * 512 * 1024 * len(steps),
        moved=8 * MIB,
    )(at, own_t, other_t, mine, other_h)


def first_sum_kernel(at_ref, *refs):
    held, outs = refs[:4], refs[4:]
    for j in range(4):
        cols = pl.ds(pl.multiple_of(lax.rem(at_ref[1] + j, 4) * 128, 128), 128)
        total = held[0][:, cols]
        for ref in held[1:]:
            total += ref[:, cols].astype(F32)
        outs[j][...] = total.astype(outs[j].dtype)


def first_sum(at, parts):
    kinds = [struct((KVW, 128), F32)] + [struct((KVW, 128), BF)] * 3
    return call(first_sum_kernel, kinds, [SM] + [VM] * 4, vmem=14, moved=6 * MIB)(at, *parts)


def second_sum_kernel(at_ref, *refs):
    held = refs[:4]
    q_out, p_out, local_out, full = refs[4:]
    zh, core = at_ref[3], at_ref[2]
    total = held[0][...]
    for ref in held[1:]:
        total += ref[...].astype(F32)
    full[...] = total.T
    mine = full[pl.ds(pl.multiple_of(core * 64, 64), 64), :]
    other = full[pl.ds(pl.multiple_of((1 - core) * 64, 64), 64), :]
    straight = zh == core
    q_out[...] = jnp.where(straight, other, mine).astype(BF)
    p_out[...] = other.astype(BF)
    local_out[...] = jnp.where(straight, mine, 0.0)


def second_sum(at, parts):
    return call(
        second_sum_kernel,
        [struct((64, KVW), BF), struct((64, KVW), BF), struct((64, KVW), F32)],
        [SM] + [VM] * 4,
        scratch=[pltpu.VMEM((128, KVW), F32)],
        moved=2 * MIB,
    )(at, *parts)


def third_sum_kernel(local, q_in, p_in, grad_out, rows_out, total_out):
    grad = local[...] + (q_in[...].astype(F32) + p_in[...].astype(F32))
    grad_out[...] = grad
    rows = jnp.sum(grad * grad, axis=1, keepdims=True)
    rows_out[...] = jnp.broadcast_to(rows, (64, 128))
    total = jnp.sum(rows, axis=0, keepdims=True)
    total_out[...] = jnp.broadcast_to(total, (8, 128))


def third_sum(local, q_in, p_in):
    return call(
        third_sum_kernel,
        [struct((64, KVW), F32), struct((64, 128), F32), struct((8, 128), F32)],
        [VM] * 3,
        moved=MIB,
    )(local, q_in, p_in)


def send_all(value, axes):
    copies = jnp.broadcast_to(value[None], (lax.axis_size(axes), *value.shape))
    return lax.all_to_all(copies, axes, 0, 0, tiled=True)


def spread_sum(value, axes):
    return jnp.sum(send_all(value, axes), axis=0)


def update_kernel(total, rows, grad, weight, state, weight_out, state_out):
    squares = total[0:1, 0:1]
    clip = jnp.minimum(1.0, 1.0 / jnp.sqrt(squares + 1e-06))
    row = lax.broadcasted_iota(jnp.int32, (64, 64), 0)
    col = lax.broadcasted_iota(jnp.int32, (64, 64), 1)
    eye = row == col
    held = jnp.sum(jnp.where(eye, state[...], 0.0), axis=1, keepdims=True)
    new = held + clip * clip * (rows[:, 0:1] * (1.0 / KVW))
    state_out[...] = jnp.sum(jnp.where(eye, new, 0.0), axis=0, keepdims=True)
    step = RATE * clip * grad[...] / (jnp.sqrt(new) + 1e-10)
    weight_out[...] = (weight[...].astype(F32) - step).astype(BF)


def update(total, rows, grad, weight, state):
    new_weight, new_state = call(
        update_kernel,
        [struct((64, KVW), BF), struct((1, 64), F32)],
        [VM] * 5,
        moved=MIB,
    )(total, rows, grad, weight, state.reshape(1, 64))
    return new_weight, new_state.reshape(64)


def input_kernel(at_ref, grad_ref, *refs):
    own, far = refs[:4], refs[4:8]
    out, held, sem = refs[8:]
    first, second, core = at_ref[0], at_ref[1], at_ref[2]
    order = sorted(((k, j) for k in range(4) for j in range(4)), key=lambda t: (max(t), t))
    copies = []
    for n, (k, j) in enumerate(order):
        weight = jnp.concatenate([own[k][j], far[j][k]], axis=0)
        value = lax.dot_general(
            grad_ref[...], weight, (((1,), (1,)), ((), ())), preferred_element_type=F32
        ).astype(BF)
        row = tile(at_ref, lax.rem(first + 4 - j, 4), lax.rem(second + 4 - k, 4))
        for i, side in enumerate((core, 1 - core)):
            held[n, i] = value[:, i * 128 : i * 128 + 128]
            cols = pl.ds(pl.multiple_of((2 * row + side) * 128, 128), 128)
            copy = pltpu.make_async_copy(held.at[n, i], out.at[:, cols], sem.at[2 * n + i])
            copy.start()
            copies.append(copy)
    for copy in copies:
        copy.wait()


def input_product(at, key_grad, own, far):
    return call(
        input_kernel,
        [struct((512, 4096), BF)],
        [SM] + [VM] * 9,
        out_specs=[ANY],
        scratch=[pltpu.VMEM((16, 2, 512, 128), BF), pltpu.SemaphoreType.DMA((32,))],
        vmem=22,
        flops=2 * 512 * 1024 * 4096,
        moved=13 * MIB,
    )(at, key_grad, *own, *far)[0]


def shards(hidden, key_weight, key_state, key_cotangent, doc_lengths):
    x, y, zh, core = (lax.axis_index(name) for name in DP)
    first = jnp.where(core == 0, x, y)
    second = jnp.where(core == 0, y, x)
    at = jnp.stack([first, second, core, zh]).astype(jnp.int32)
    straight = zh == core

    mine, other_h = split(at, hidden)
    other_h = swap_cores(other_h)
    turned = rope(doc_lengths, key_cotangent)
    other_t = swap_cores(turned)

    part2, part1 = grad_parts((2, 1), at, turned, other_t, mine, other_h)
    part3, part0 = grad_parts((3, 0), at, turned, other_t, mine, other_h)
    parts = [part0] + [spread(v, j) for j, v in ((1, part1), (2, part2), (3, part3))]

    kept, _ = lax.optimization_barrier((turned, part0))
    key_grad = turn_back(kept)

    weight, _ = lax.optimization_barrier((key_weight, part0))
    q_w = lax.ppermute(weight, ("zh", "c"), [(0, 2), (1, 0), (2, 3), (3, 1)])
    p_w = lax.ppermute(weight, ("zh", "c"), [(1, 2), (2, 1)])
    same = jnp.where(straight, key_weight, q_w)
    cross = jnp.where(straight, q_w, p_w)
    rows = jnp.concatenate(
        [jnp.where(core == 0, same, cross), jnp.where(core == 0, cross, same)], axis=0
    )

    near = [spread(rows, 1), spread(rows, 3)]
    parts[0], rows, key_grad, *near = lax.optimization_barrier((parts[0], rows, key_grad, *near))

    sums = first_sum(at, parts)
    ring = [rows, near[0], spread(rows, 2), near[1]]
    sums = [sums[0]] + [spread_across(sums[j], j) for j in (1, 2, 3)]
    q_out, p_out, local = second_sum(at, sums)
    q_in = lax.ppermute(q_out, ("zh", "c"), [(0, 1), (1, 3), (2, 0), (3, 2)])
    p_in = lax.ppermute(p_out, ("zh", "c"), [(2, 1), (1, 2)])

    *ring, _ = lax.optimization_barrier((*ring, q_out))
    cat = jnp.stack(ring)
    own = [cat] + [spread_across(cat, j) for j in (1, 2, 3)]

    grad, squares, total = third_sum(local, q_in, p_in)
    far = [swap_cores(cat)]
    total = lax.psum(total, "c")
    total = spread_sum(total, ("zh", "mp"))
    *rest, total = lax.optimization_barrier((*own[1:], total))
    far += [swap_cores(v) for v in rest]
    own = [cat, *rest]
    everywhere = send_all(total, ("x", "y"))
    input_grad = input_product(at, key_grad, own, far)
    input_grad, everywhere = lax.optimization_barrier((input_grad, everywhere))
    total = jnp.sum(everywhere, axis=0)
    new_weight, new_state = update(total, squares, grad, key_weight, key_state)
    return (input_grad, new_weight, new_state)


def solution(mesh):
    finer = Mesh(mesh.devices.reshape(4, 4, 2, 2, mesh.shape["mp"]), (*DP, "mp"))
    placed = (P(DP, "mp"), P(MP_DP, None), P(MP_DP), P(DP, None), P(DP, None))
    return jax.shard_map(
        shards,
        mesh=finer,
        in_specs=placed,
        out_specs=(P(DP, "mp"), P(MP_DP, None), P(MP_DP)),
        check_vma=False,
    )
```

```python
import functools

import jax
import jax.numpy as jnp
from jax import lax
from jax.experimental import pallas as pl
from jax.experimental.pallas import tpu as pltpu
from jax.sharding import Mesh
from jax.sharding import PartitionSpec as P

HD = 128
LEN = 256
KVW = 1024
HALF = 512
DP = ("x", "y", "zh", "c")
MP_DP = ("mp", "x", "y", "zh", "c")
RATE = 0.01
BF = jnp.bfloat16
F32 = jnp.float32
VM = pl.BlockSpec(memory_space=pltpu.VMEM)
SM = pl.BlockSpec(memory_space=pltpu.SMEM)
ANY = pl.BlockSpec(memory_space=pl.ANY)
MIB = 1 << 20


def call(body, outs, in_specs, out_specs=None, scratch=(), vmem=8, flops=0, moved=0, alias=None):
    return pl.pallas_call(
        body,
        out_shape=outs,
        in_specs=in_specs,
        out_specs=[VM] * len(outs) if out_specs is None else out_specs,
        scratch_shapes=list(scratch),
        input_output_aliases=alias or {},
        compiler_params=pltpu.CompilerParams(vmem_limit_bytes=vmem * MIB),
        cost_estimate=pl.CostEstimate(flops=flops, bytes_accessed=moved, transcendentals=0),
    )


def struct(shape, dtype):
    return jax.ShapeDtypeStruct(shape, dtype)


def spread(value, by):
    pairs = []
    for x in range(4):
        for y in range(4):
            here = (4 * x + y) * 2
            pairs.append((here, (4 * ((x + by) % 4) + y) * 2))
            pairs.append((here + 1, (4 * x + (y + by) % 4) * 2 + 1))
    return lax.ppermute(value, ("x", "y", "c"), pairs)


def spread_across(value, by):
    pairs = []
    for x in range(4):
        for y in range(4):
            here = (4 * x + y) * 2
            pairs.append((here, (4 * x + (y + by) % 4) * 2))
            pairs.append((here + 1, (4 * ((x + by) % 4) + y) * 2 + 1))
    return lax.ppermute(value, ("x", "y", "c"), pairs)


def swap_cores(value):
    return lax.ppermute(value, "c", [(0, 1), (1, 0)])


def rope_kernel(len_ref, cot_ref, turned_ref):
    lane = lax.broadcasted_iota(jnp.int32, (LEN, HD), 1)
    place = lax.broadcasted_iota(jnp.int32, (LEN, HD), 0)
    index = jnp.where(lane < HD // 2, lane, lane - HD // 2).astype(F32)
    frequency = jnp.exp(-(2.0 * index / HD) * jnp.log(jnp.full((LEN, HD), 500000.0, F32)))
    row = lax.broadcasted_iota(jnp.int32, (HD, HD), 0)
    col = lax.broadcasted_iota(jnp.int32, (HD, HD), 1)
    eye = (row == col).astype(F32).astype(BF)
    far = jnp.where(col < HD // 2, col + HD // 2, col - HD // 2)
    swap = (row == far).astype(F32).astype(BF)
    for seq in range(2):
        start = jnp.int32(0)
        first = jnp.zeros((LEN, HD), jnp.int32)
        for doc in range(1, 4):
            start = start + len_ref[seq, doc - 1]
            first = jnp.where(place >= start, start, first)
        angle = (place - first).astype(F32) * frequency
        both = jnp.cos(jnp.where(lane < HD // 2, angle, angle - 1.5707963267948966))
        turned_over = pltpu.roll(both, HD // 2, 1)
        cos = jnp.where(lane < HD // 2, both, turned_over)
        sin = jnp.where(lane < HD // 2, turned_over, -both)
        rows = pl.ds(seq * LEN, LEN)
        for head in range(KVW // HD):
            cols = pl.ds(head * HD, HD)
            value = cot_ref[rows, cols]
            swapped = jnp.dot(value, swap, preferred_element_type=F32)
            out = (value.astype(F32) * cos + swapped * sin).astype(BF)
            turned = lax.dot_general(
                eye, out, (((1,), (1,)), ((), ())), preferred_element_type=F32
            )
            turned_ref[cols, rows] = turned.astype(BF)


def rope(doc_lengths, cotangent):
    return call(
        rope_kernel,
        [struct((KVW, 512), BF)],
        [SM, VM],
        vmem=12,
        moved=3 * MIB,
    )(doc_lengths, cotangent)[0]


def turn_back_kernel(turned_ref, grad_ref):
    row = lax.broadcasted_iota(jnp.int32, (256, 256), 0)
    col = lax.broadcasted_iota(jnp.int32, (256, 256), 1)
    eye = (row == col).astype(F32).astype(BF)
    for seq in range(2):
        rows = slice(seq * LEN, seq * LEN + LEN)
        value = lax.dot_general(
            eye, turned_ref[:, rows], (((1,), (1,)), ((), ())), preferred_element_type=F32
        )
        grad_ref[rows, :] = value.astype(BF)


def turn_back(turned):
    return call(
        turn_back_kernel, [struct((512, KVW), BF)], [VM], vmem=12, moved=2 * MIB
    )(turned)[0]


def split_kernel(at_ref, hidden_ref, mine, other):
    core = at_ref[2]
    for j in range(16):
        here = pl.ds(j * 128, 128)
        mine[:, here] = hidden_ref[:, pl.ds(pl.multiple_of((2 * j + core) * 128, 128), 128)]
        other[:, here] = hidden_ref[:, pl.ds(pl.multiple_of((2 * j + 1 - core) * 128, 128), 128)]


def split(at, hidden):
    half = pl.BlockSpec((256, 2048), lambda i: (i, 0))
    return pl.pallas_call(
        split_kernel,
        grid=(2,),
        in_specs=[SM, pl.BlockSpec((256, 4096), lambda i: (i, 0))],
        out_specs=[half, half],
        out_shape=[struct((512, 2048), BF)] * 2,
        compiler_params=pltpu.CompilerParams(vmem_limit_bytes=16 * MIB),
        cost_estimate=pl.CostEstimate(flops=0, bytes_accessed=8 * MIB, transcendentals=0),
    )(at, hidden)


def tile(at_ref, first, second):
    core = at_ref[2]
    return first * jnp.where(core == 0, 4, 1) + second * jnp.where(core == 0, 1, 4)


def grad_kernel(steps, at_ref, own_t, other_t, mine, other_h, *outs):
    first = at_ref[0]
    for j, out in zip(steps, outs):
        to = lax.rem(first + j, 4)
        tiles = [pl.ds(pl.multiple_of(tile(at_ref, to, i) * 128, 128), 128) for i in range(4)]
        for half in (0, 1):
            pair = tiles[2 * half : 2 * half + 2]
            right = jnp.concatenate(
                [jnp.concatenate([h[:, t] for t in pair], axis=1) for h in (mine, other_h)],
                axis=0,
            )
            for part in (0, 1):
                rows = slice(part * HALF, part * HALF + HALF)
                left = jnp.concatenate([own_t[rows, :], other_t[rows, :]], axis=1)
                value = jnp.dot(left, right, preferred_element_type=F32)
                out[rows, half * 256 : half * 256 + 256] = value.astype(out.dtype)


def grad_parts(steps, at, own_t, other_t, mine, other_h):
    outs = [struct((KVW, 512), BF if j else F32) for j in steps]
    return call(
        functools.partial(grad_kernel, steps),
        outs,
        [SM, VM, VM, VM, VM],
        vmem=20,
        flops=2 * 1024 * 512 * 1024 * len(steps),
        moved=8 * MIB,
    )(at, own_t, other_t, mine, other_h)


def first_sum_kernel(at_ref, *refs):
    held, outs = refs[:4], refs[4:]
    for j in range(4):
        cols = pl.ds(pl.multiple_of(lax.rem(at_ref[1] + j, 4) * 128, 128), 128)
        total = held[0][:, cols]
        for ref in held[1:]:
            total += ref[:, cols].astype(F32)
        outs[j][...] = total.astype(outs[j].dtype)


def first_sum(at, parts):
    kinds = [struct((KVW, 128), F32)] + [struct((KVW, 128), BF)] * 3
    return call(first_sum_kernel, kinds, [SM] + [VM] * 4, vmem=14, moved=6 * MIB)(at, *parts)


def second_sum_kernel(at_ref, *refs):
    held = refs[:4]
    q_out, p_out, local_out, full = refs[4:]
    zh, core = at_ref[3], at_ref[2]
    total = held[0][...]
    for ref in held[1:]:
        total += ref[...].astype(F32)
    full[...] = total.T
    mine = full[pl.ds(pl.multiple_of(core * 64, 64), 64), :]
    other = full[pl.ds(pl.multiple_of((1 - core) * 64, 64), 64), :]
    straight = zh == core
    q_out[...] = jnp.where(straight, other, mine).astype(BF)
    p_out[...] = other.astype(BF)
    local_out[...] = jnp.where(straight, mine, 0.0)


def second_sum(at, parts):
    return call(
        second_sum_kernel,
        [struct((64, KVW), BF), struct((64, KVW), BF), struct((64, KVW), F32)],
        [SM] + [VM] * 4,
        scratch=[pltpu.VMEM((128, KVW), F32)],
        moved=2 * MIB,
    )(at, *parts)


def third_sum_kernel(local, q_in, p_in, grad_out, rows_out, total_out):
    grad = local[...] + (q_in[...].astype(F32) + p_in[...].astype(F32))
    grad_out[...] = grad
    rows = jnp.sum(grad * grad, axis=1, keepdims=True)
    rows_out[...] = jnp.broadcast_to(rows, (64, 128))
    total = jnp.sum(rows, axis=0, keepdims=True)
    total_out[...] = jnp.broadcast_to(total, (8, 128))


def third_sum(local, q_in, p_in):
    return call(
        third_sum_kernel,
        [struct((64, KVW), F32), struct((64, 128), F32), struct((8, 128), F32)],
        [VM] * 3,
        moved=MIB,
    )(local, q_in, p_in)


def send_all(value, axes):
    copies = jnp.broadcast_to(value[None], (lax.axis_size(axes), *value.shape))
    return lax.all_to_all(copies, axes, 0, 0, tiled=True)


def spread_sum(value, axes):
    return jnp.sum(send_all(value, axes), axis=0)


def update_kernel(total, rows, grad, weight, state, weight_out, state_out):
    squares = total[0:1, 0:1]
    clip = jnp.minimum(1.0, 1.0 / jnp.sqrt(squares + 1e-06))
    row = lax.broadcasted_iota(jnp.int32, (64, 64), 0)
    col = lax.broadcasted_iota(jnp.int32, (64, 64), 1)
    eye = row == col
    held = jnp.sum(jnp.where(eye, state[...], 0.0), axis=1, keepdims=True)
    new = held + clip * clip * (rows[:, 0:1] * (1.0 / KVW))
    state_out[...] = jnp.sum(jnp.where(eye, new, 0.0), axis=0, keepdims=True)
    step = RATE * clip * grad[...] / (jnp.sqrt(new) + 1e-10)
    weight_out[...] = (weight[...].astype(F32) - step).astype(BF)


def update(total, rows, grad, weight, state):
    new_weight, new_state = call(
        update_kernel,
        [struct((64, KVW), BF), struct((1, 64), F32)],
        [VM] * 5,
        moved=MIB,
    )(total, rows, grad, weight, state.reshape(1, 64))
    return new_weight, new_state.reshape(64)


def input_kernel(at_ref, grad_ref, *refs):
    own, far = refs[:4], refs[4:8]
    out, held, sem = refs[8:]
    first, second, core = at_ref[0], at_ref[1], at_ref[2]
    order = sorted(((k, j) for k in range(4) for j in range(4)), key=lambda t: (max(t), t))
    copies = []
    for n, (k, j) in enumerate(order):
        weight = jnp.concatenate([own[k][j], far[j][k]], axis=0)
        value = lax.dot_general(
            grad_ref[...], weight, (((1,), (1,)), ((), ())), preferred_element_type=F32
        ).astype(BF)
        row = tile(at_ref, lax.rem(first + 4 - j, 4), lax.rem(second + 4 - k, 4))
        for i, side in enumerate((core, 1 - core)):
            held[n, i] = value[:, i * 128 : i * 128 + 128]
            cols = pl.ds(pl.multiple_of((2 * row + side) * 128, 128), 128)
            copy = pltpu.make_async_copy(held.at[n, i], out.at[:, cols], sem.at[2 * n + i])
            copy.start()
            copies.append(copy)
    for copy in copies:
        copy.wait()


def input_product(at, key_grad, own, far):
    return call(
        input_kernel,
        [struct((512, 4096), BF)],
        [SM] + [VM] * 9,
        out_specs=[ANY],
        scratch=[pltpu.VMEM((16, 2, 512, 128), BF), pltpu.SemaphoreType.DMA((32,))],
        vmem=22,
        flops=2 * 512 * 1024 * 4096,
        moved=13 * MIB,
    )(at, key_grad, *own, *far)[0]


def shards(hidden, key_weight, key_state, key_cotangent, doc_lengths):
    x, y, zh, core = (lax.axis_index(name) for name in DP)
    first = jnp.where(core == 0, x, y)
    second = jnp.where(core == 0, y, x)
    at = jnp.stack([first, second, core, zh]).astype(jnp.int32)
    straight = zh == core

    mine, other_h = split(at, hidden)
    other_h = swap_cores(other_h)
    turned = rope(doc_lengths, key_cotangent)
    other_t = swap_cores(turned)

    part2, part1 = grad_parts((2, 1), at, turned, other_t, mine, other_h)
    part3, part0 = grad_parts((3, 0), at, turned, other_t, mine, other_h)
    parts = [part0] + [spread(v, j) for j, v in ((1, part1), (2, part2), (3, part3))]

    kept, _ = lax.optimization_barrier((turned, part0))
    key_grad = turn_back(kept)

    weight, _ = lax.optimization_barrier((key_weight, part0))
    q_w = lax.ppermute(weight, ("zh", "c"), [(0, 2), (1, 0), (2, 3), (3, 1)])
    p_w = lax.ppermute(weight, ("zh", "c"), [(1, 2), (2, 1)])
    same = jnp.where(straight, key_weight, q_w)
    cross = jnp.where(straight, q_w, p_w)
    rows = jnp.concatenate(
        [jnp.where(core == 0, same, cross), jnp.where(core == 0, cross, same)], axis=0
    )

    near = [spread(rows, 1), spread(rows, 3)]
    parts[0], rows, key_grad, *near = lax.optimization_barrier((parts[0], rows, key_grad, *near))

    sums = first_sum(at, parts)
    ring = [rows, near[0], spread(rows, 2), near[1]]
    sums = [sums[0]] + [spread_across(sums[j], j) for j in (1, 2, 3)]
    q_out, p_out, local = second_sum(at, sums)
    q_in = lax.ppermute(q_out, ("zh", "c"), [(0, 1), (1, 3), (2, 0), (3, 2)])
    p_in = lax.ppermute(p_out, ("zh", "c"), [(2, 1), (1, 2)])

    *ring, _ = lax.optimization_barrier((*ring, q_out))
    cat = jnp.stack(ring)
    own = [cat] + [spread_across(cat, j) for j in (1, 2, 3)]

    grad, squares, total = third_sum(local, q_in, p_in)
    far = [swap_cores(cat)]
    total = lax.psum(total, "c")
    total = spread_sum(total, ("zh", "mp"))
    *rest, total = lax.optimization_barrier((*own[1:], total))
    far += [swap_cores(v) for v in rest]
    own = [cat, *rest]
    everywhere = send_all(total, ("x", "y"))
    input_grad = input_product(at, key_grad, own, far)
    input_grad, everywhere = lax.optimization_barrier((input_grad, everywhere))
    total = jnp.sum(everywhere, axis=0)
    new_weight, new_state = update(total, squares, grad, key_weight, key_state)
    return (input_grad, new_weight, new_state)


def solution(mesh):
    finer = Mesh(mesh.devices.reshape(4, 4, 2, 2, mesh.shape["mp"]), (*DP, "mp"))
    placed = (P(DP, "mp"), P(MP_DP, None), P(MP_DP), P(DP, None), P(DP, None))
    return jax.shard_map(
        shards,
        mesh=finer,
        in_specs=placed,
        out_specs=(P(DP, "mp"), P(MP_DP, None), P(MP_DP)),
        check_vma=False,
    )
```
